32 devices in a mesh: grp: 4 (over y, x), seq: 8 (over z, core).
Axes of the slice: x: 2, y: 2, z: 4, core: 2. Of those that a mesh axis runs over, the one named last changes fastest.
Arguments:
- tokens: bfloat16 [4, 3072, 1536], P('grp', 'seq'), may hold values from -32 to 32, as said below
- router: bfloat16 [1536, 128], P('grp'), may hold values from -1 to 1, as said below
- norm_gain: float32 [8, 1536], P('seq'), may hold values from 0.1 to 1.9
- w_in: bfloat16 [8, 1536, 6144], P('seq', None, 'grp'), may hold values from -0.15625 to 0.15625
- w_out: bfloat16 [8, 6144, 1536], P('seq', 'grp'), may hold values from -0.078125 to 0.078125
Outputs:
- output: bfloat16 [4, 3072, 1536], P('grp', 'seq')
The draws below stay inside these ranges and needn't reach their ends.
Inputs may be any that keep to these rules, and one draw needn't show every extreme that they name: `tokens`: token features are real values. `router`: slot parameters are real values.
All inputs are finite; a program needn't handle non-finite values.
Results may differ from the reference program's by a relative error of at most 0.0075.
Values may be sent and summed in bfloat16 or wider, within the bound.
A program may use at most 64 MiB of HBM per device.

```python
import math
import jax
import jax.numpy as jnp
from jax import lax

D = 1536
FF = 6144
SLOT_EXP = 16
EXPERTS = 8
SLOTS = 128
GROUPS = 4
TOKENS = 3072
FF_DEV = 1536
N_GRP = 4


def joint_draw(key):
    base = jax.random.fold_in(key, 4711)
    keys = jax.random.split(base, 2)
    feats = jax.random.normal(keys[0], (GROUPS, TOKENS, D), jnp.float32)
    mixer = jnp.clip(jax.random.normal(keys[1], (D, SLOTS), jnp.float32), -4.0, 4.0) * (2.5 / math.sqrt(D))
    limit = 1.0 + 400 // D
    feats = jnp.clip(feats, -6.0, 6.0)
    mixer = jnp.clip(mixer, -limit, limit)
    return (feats, mixer)


def draw_tokens(key, part):
    return joint_draw(key)[0].astype(jnp.bfloat16)


def draw_router(key, part):
    return joint_draw(key)[1].astype(jnp.bfloat16)


def block_levels(own_key, dims, pieces, low, top_value):
    def one(axis_at, shards_of):
        steps = jax.random.uniform(jax.random.fold_in(jax.random.fold_in(own_key, 6), axis_at), (shards_of,), jnp.float32, low / len(pieces), top_value / len(pieces))
        return jnp.repeat(jnp.exp(steps), dims[axis_at] // shards_of).reshape((-1,) + (1,) * (len(dims) - axis_at - 1))

    factor_of = one(*pieces[0])
    for cut in pieces[1:]:
        factor_of = factor_of * one(*cut)
    return factor_of


def gaussian(stream_key, extent, width, most, pieces=(), dtype=jnp.bfloat16):
    factor_of = block_levels(stream_key, extent, pieces, -0.22, 0.18) if pieces else 1.0
    entries = jax.random.normal(stream_key, extent, jnp.float32) * width * factor_of
    return jnp.minimum(jnp.maximum(entries, -most), most).astype(dtype)


def setup_inputs(seed: int = 0) -> dict:
    splits = jax.random.split(jax.random.key(seed), 6)
    tokens = draw_tokens(jax.random.fold_in(splits[5], 71), 0)
    router = draw_router(jax.random.fold_in(splits[5], 71), 0)
    norm_gain = jnp.clip(1.0 + 0.18 * jax.random.normal(splits[2], (EXPERTS, D), jnp.float32), 0.1, 1.9)
    w_in = gaussian(splits[3], (EXPERTS, D, FF), D ** -0.5, 0.15625, ((0, 8), (2, 4)))
    w_out = gaussian(splits[4], (EXPERTS, FF, D), FF ** -0.5, 0.078125, ((0, 8), (1, 4)))
    return {"tokens": tokens, "router": router, "norm_gain": norm_gain, "w_in": w_in, "w_out": w_out}


def reference(tokens, router, norm_gain, w_in, w_out):

    def dispatch_group(feats):
        logits = jnp.dot(feats, router, preferred_element_type=jnp.float32)
        highest = lax.optimization_barrier(jnp.max(logits, axis=0, keepdims=True))
        dispatch = jnp.exp(logits - highest).astype(jnp.bfloat16)
        return jnp.dot(dispatch.T, feats, preferred_element_type=jnp.float32)
    pooled = lax.map(dispatch_group, tokens)
    pooled = pooled.reshape(GROUPS, EXPERTS, SLOT_EXP, D)
    mean_sq = lax.optimization_barrier(jnp.mean(pooled * pooled, axis=-1, keepdims=True))
    slots = (pooled * lax.rsqrt(mean_sq + 1e-06) * norm_gain[None, :, None, :]).astype(jnp.bfloat16)

    def run_expert(operands):
        expert_slots, weight_in, weight_out = operands
        gathered = expert_slots.reshape(GROUPS * SLOT_EXP, D)
        hidden = jax.nn.gelu(jnp.dot(gathered, weight_in, preferred_element_type=jnp.float32)).astype(jnp.bfloat16)
        blocks = hidden.reshape(GROUPS * SLOT_EXP, N_GRP, FF_DEV).transpose(1, 0, 2).astype(jnp.float32)
        out_blocks = weight_out.reshape(N_GRP, FF_DEV, D).astype(jnp.float32)
        parts = jnp.einsum('krf,kfd->krd', blocks, out_blocks, precision=lax.Precision.HIGHEST)
        rounded = lax.optimization_barrier(parts.astype(jnp.bfloat16)).astype(jnp.float32)
        return lax.optimization_barrier(jnp.sum(rounded, axis=0)).astype(jnp.bfloat16).reshape(GROUPS, SLOT_EXP, D)
    expert_out = lax.map(run_expert, (slots.transpose(1, 0, 2, 3), w_in, w_out))
    expert_out = expert_out.transpose(1, 0, 2, 3).reshape(GROUPS, SLOTS, D)

    def combine_group(operands):
        feats, outputs = operands
        logits = jnp.dot(feats, router, preferred_element_type=jnp.float32)
        weights = jax.nn.softmax(logits, axis=1).astype(jnp.bfloat16)
        mixed = jnp.dot(weights, outputs, preferred_element_type=jnp.float32)
        return (feats.astype(jnp.float32) + mixed).astype(jnp.bfloat16)
    return lax.map(combine_group, (tokens, expert_out))
```

```python
import functools

import jax
import jax.numpy as jnp
from jax import lax
from jax.experimental import pallas as pl
from jax.experimental.pallas import tpu as pltpu
from jax.sharding import PartitionSpec as P

F32, BF16 = jnp.float32, jnp.bfloat16
LANES = 128


def tile_of(n):
    for t in (512, 384, 256, 128):
        if n % t == 0:
            return t
    return n


def remote(src, dst, send, recv, g, e):
    return pltpu.make_async_remote_copy(
        src_ref=src, dst_ref=dst, send_sem=send, recv_sem=recv,
        device_id={"grp": g, "seq": e}, device_id_type=pl.DeviceIdType.MESH,
    )


def kernel(G, S, tok_h, rt_h, gain, wi_h, wo_h, eo, wts,
           tok, rt, wi, wo, logits, dT, pf, pb, xb, hp, hpc, hz, hzc, cown, sb, zb,
           pool, gath, hid, part, rs, eown,
           loc, a_s, a_r, f_s, f_r, p_s, p_r, h_s, h_r, z_s, z_r, zh_s, zh_r,
           n_s, n_r, r_s, r_r, e_s, e_r, ef_s, ef_r):
    g, e = lax.axis_index("grp"), lax.axis_index("seq")
    Z = S // 2
    z, k = e // 2, e % 2
    partner = e + 1 - 2 * k
    rows = rt_h.shape[0]
    half = rows // 2
    T, D = tok.shape
    SL = rt.shape[1]
    E = SL // S
    FF = wi.shape[1]
    tn = tile_of(D)
    NT = D // tn
    tf = tile_of(FF)
    cols = [pl.ds(t * tn, tn) for t in range(NT)]

    def rsl(gg, kk):
        return pl.ds(pl.multiple_of(gg * rows + kk * half, 16), half)

    c_rt = pltpu.make_async_copy(rt_h, rt.at[pl.ds(pl.multiple_of(g * rows, 16), rows)], loc.at[0])
    c_tok = pltpu.make_async_copy(tok_h.at[0], tok, loc.at[1])
    c_wi = pltpu.make_async_copy(wi_h.at[0], wi, loc.at[2])
    c_wo = pltpu.make_async_copy(wo_h.at[0], wo, loc.at[3])
    c_rt.start()
    c_tok.start()
    hp[...] = jnp.zeros_like(hp)
    hz[...] = jnp.zeros_like(hz)

    bar = pltpu.get_barrier_semaphore()

    def greet(gg, ee):
        pl.semaphore_signal(bar, inc=1, device_id={"grp": gg, "seq": ee},
                            device_id_type=pl.DeviceIdType.MESH)

    def gpeer(d):
        return lax.rem(g + d, G)

    def gfrom(d):
        return lax.rem(g - d + G, G)

    def zpeer(d):
        return lax.rem(z + d, Z)

    def zfrom(d):
        return lax.rem(z - d + Z, Z)

    greet(g, partner)
    for d in range(1, G):
        greet(gpeer(d), e)
    for d in range(1, Z):
        greet(g, zpeer(d) * 2 + k)
    pl.semaphore_wait(bar, G + Z - 1)

    pend = []

    ksl = pl.ds(pl.multiple_of(k * half, 16), half)
    for d in range(1, G):
        c = remote(rt_h.at[ksl], rt.at[rsl(g, k)], a_s.at[d], a_r.at[d], gpeer(d), e)
        c.start()
        pend.append(c)
    c_wi.start()
    c_wo.start()
    for d in range(1, G):
        sl = rt.at[rsl(gfrom(d), k)]
        remote(sl, sl, a_s.at[d], a_r.at[d], g, partner).wait_recv()
        c = remote(sl, sl, f_s.at[d], f_r.at[d], g, partner)
        c.start()
        pend.append(c)
    for d in range(1, G):
        sl = rt.at[rsl(gfrom(d), 1 - k)]
        remote(sl, sl, f_s.at[d], f_r.at[d], g, partner).wait_recv()
    c_rt.wait()
    c_tok.wait()

    lg = jnp.dot(tok[...], rt[...], preferred_element_type=F32)
    high = jnp.max(lg, axis=0, keepdims=True)
    hp[0:1] = high
    c_h = remote(hp.at[pl.ds(0, 1)], hp.at[pl.ds(1, 1)], h_s, h_r, g, partner)
    c_h.start()
    pend.append(c_h)
    logits[...] = lg
    dT[...] = jnp.transpose(jnp.exp(lg - high)).astype(BF16)

    pair = []
    for t in range(NT):
        ps = jnp.dot(dT[...], tok[:, cols[t]], preferred_element_type=F32).reshape(Z, 2, E, tn)
        pf[:, :, :, cols[t]] = ps
        pb[:, :, :, cols[t]] = ps.astype(BF16)
        c = remote(pb.at[:, 1 - k, :, cols[t]], xb.at[:, :, cols[t]], p_s.at[t], p_r.at[t], g, partner)
        c.start()
        pair.append(c)

    c_h.wait_recv()
    hh = hp[...]
    hm = jnp.maximum(hh[0:1], hh[1:2])
    hpc[...] = jnp.transpose(jnp.exp(jnp.minimum(hh - hm, 0.0))).reshape(Z, 2, E, LANES)
    hz[0:1] = hm
    for d in range(1, Z):
        c = remote(hz.at[pl.ds(0, 1)], hz.at[pl.ds(d, 1)], zh_s.at[d], zh_r.at[d], g, zpeer(d) * 2 + k)
        c.start()
        pend.append(c)
    for t in range(NT):
        pair[t].wait_recv()
        for d in range(Z - 1, -1, -1):
            zz = zpeer(d)
            fac = hpc[zz, k]
            v = pf[zz, k, :, cols[t]] * fac[:, 0:1] + xb[zz, :, cols[t]].astype(F32) * fac[:, 1:2]
            if d == 0:
                cown[:, cols[t]] = v
            else:
                sb[d, :, cols[t]] = v.astype(BF16)
                c = remote(sb.at[d, :, cols[t]], zb.at[d, :, cols[t]], z_s.at[d, t], z_r.at[d, t],
                           g, zz * 2 + k)
                c.start()
                pend.append(c)
    for c in pair:
        c.wait_send()

    lg = logits[...]
    ex = jnp.exp(lg - jnp.max(lg, axis=1, keepdims=True))
    wts[...] = (ex / jnp.sum(ex, axis=1, keepdims=True)).astype(BF16)

    for d in range(1, Z):
        sl = hz.at[pl.ds(d, 1)]
        remote(sl, sl, zh_s.at[d], zh_r.at[d], g, e).wait_recv()
    hh = hz[...]
    top = jnp.max(hh[0:Z], axis=0, keepdims=True)
    hzc[...] = jnp.transpose(jnp.exp(jnp.minimum(hh - top, 0.0))).reshape(S, E, LANES)
    fac = hzc[e]
    sq = jnp.zeros((E, 1), F32)
    for t in range(NT):
        v = cown[:, cols[t]] * fac[:, 0:1]
        for d in range(1, Z):
            sl = zb.at[d, :, cols[t]]
            remote(sl, sl, z_s.at[d, t], z_r.at[d, t], g, e).wait_recv()
            v = v + zb[d, :, cols[t]].astype(F32) * fac[:, d:d + 1]
        pool[:, cols[t]] = v
        sq = sq + jnp.sum(v * v, axis=1, keepdims=True)
    inv = lax.rsqrt(sq / D + 1e-06)
    gath[g] = (pool[...] * inv * gain[...]).astype(BF16)
    for d in range(1, G):
        c = remote(gath.at[g], gath.at[g], n_s.at[d], n_r.at[d], gpeer(d), e)
        c.start()
        pend.append(c)
    c_wi.wait()
    c_wo.wait()
    for d in range(1, G):
        sl = gath.at[gfrom(d)]
        remote(sl, sl, n_s.at[d], n_r.at[d], g, e).wait_recv()

    x = gath[...].reshape(G * E, D)
    for t in range(FF // tf):
        fs = pl.ds(t * tf, tf)
        hid[:, fs] = jax.nn.gelu(jnp.dot(x, wi[:, fs], preferred_element_type=F32)).astype(BF16)
    hd = hid[...]
    for t in range(NT):
        part[:, :, cols[t]] = jnp.dot(hd, wo[:, cols[t]], preferred_element_type=F32).astype(BF16).reshape(G, E, tn)
        for d in range(1, G):
            c = remote(part.at[gpeer(d), :, cols[t]], rs.at[d, :, cols[t]], r_s.at[d, t], r_r.at[d, t],
                       gpeer(d), e)
            c.start()
            pend.append(c)

    own = []
    for t in range(NT):
        v = part[g, :, cols[t]].astype(F32)
        for d in range(1, G):
            sl = rs.at[d, :, cols[t]]
            remote(sl, sl, r_s.at[d, t], r_r.at[d, t], g, e).wait_recv()
            v = v + rs[d, :, cols[t]].astype(F32)
        eown[:, cols[t]] = v.astype(BF16)
        src, dst = eown.at[:, cols[t]], eo.at[e, :, cols[t]]
        for d in range(Z - 1, 0, -1):
            c = remote(src, dst, e_s.at[d, t], e_r.at[d, t], g, zpeer(d) * 2 + k)
            c.start()
            pend.append(c)
        c = remote(src, dst, ef_s.at[0, t], ef_r.at[0, t], g, partner)
        c.start()
        pend.append(c)
        c = pltpu.make_async_copy(src, dst, e_s.at[0, t])
        c.start()
        own.append(c)
    for t in range(NT):
        for d in range(1, Z):
            sl = eo.at[zfrom(d) * 2 + k, :, cols[t]]
            remote(sl, sl, e_s.at[d, t], e_r.at[d, t], g, e).wait_recv()
            c = remote(sl, sl, ef_s.at[d, t], ef_r.at[d, t], g, partner)
            c.start()
            pend.append(c)
    for t in range(NT):
        own[t].wait()
        for d in range(Z):
            sl = eo.at[zfrom(d) * 2 + 1 - k, :, cols[t]]
            remote(sl, sl, ef_s.at[d, t], ef_r.at[d, t], g, e).wait_recv()
    for c in pend:
        c.wait_send()


def local(G, S, tokens, router, norm_gain, w_in, w_out):
    _, T, D = tokens.shape
    rows, SL = router.shape
    E, Z = SL // S, S // 2
    FF = w_in.shape[2]
    NT = D // tile_of(D)
    anyspace = pl.BlockSpec(memory_space=pl.ANY)
    vmem = pl.BlockSpec(memory_space=pltpu.VMEM)
    dma = lambda *s: pltpu.SemaphoreType.DMA(s)
    eo, wts = pl.pallas_call(
        functools.partial(kernel, G, S),
        out_shape=(jax.ShapeDtypeStruct((S, E, D), BF16), jax.ShapeDtypeStruct((T, SL), BF16)),
        in_specs=[anyspace, anyspace, vmem, anyspace, anyspace],
        out_specs=(anyspace, vmem),
        scratch_shapes=[
            pltpu.VMEM((T, D), BF16),
            pltpu.VMEM((rows * G, SL), BF16),
            pltpu.VMEM((D, FF), BF16),
            pltpu.VMEM((FF, D), BF16),
            pltpu.VMEM((T, SL), F32),
            pltpu.VMEM((SL, T), BF16),
            pltpu.VMEM((Z, 2, E, D), F32),
            pltpu.VMEM((Z, 2, E, D), BF16),
            pltpu.VMEM((Z, E, D), BF16),
            pltpu.VMEM((LANES, SL), F32),
            pltpu.VMEM((Z, 2, E, LANES), F32),
            pltpu.VMEM((LANES, SL), F32),
            pltpu.VMEM((S, E, LANES), F32),
            pltpu.VMEM((E, D), F32),
            pltpu.VMEM((Z, E, D), BF16),
            pltpu.VMEM((Z, E, D), BF16),
            pltpu.VMEM((E, D), F32),
            pltpu.VMEM((G, E, D), BF16),
            pltpu.VMEM((G * E, FF), BF16),
            pltpu.VMEM((G, E, D), BF16),
            pltpu.VMEM((G, E, D), BF16),
            pltpu.VMEM((E, D), BF16),
            dma(4), dma(G), dma(G), dma(G), dma(G), dma(NT), dma(NT),
            pltpu.SemaphoreType.DMA, pltpu.SemaphoreType.DMA,
            dma(Z, NT), dma(Z, NT), dma(Z), dma(Z),
            dma(G), dma(G), dma(G, NT), dma(G, NT),
            dma(Z, NT), dma(Z, NT), dma(Z, NT), dma(Z, NT),
        ],
        compiler_params=pltpu.CompilerParams(
            collective_id=0, has_side_effects=True, vmem_limit_bytes=48 * 1024 * 1024
        ),
    )(tokens, router, norm_gain, w_in, w_out)
    mixed = jnp.dot(wts, eo.reshape(SL, D), preferred_element_type=F32)
    return (tokens[0].astype(F32) + mixed).astype(BF16)[None]


def solution(mesh):
    in_specs = (
        P("grp", "seq", None),
        P("grp", None),
        P("seq", None),
        P("seq", None, "grp"),
        P("seq", "grp", None),
    )
    out_specs = P("grp", "seq", None)
    f = functools.partial(local, mesh.shape["grp"], mesh.shape["seq"])
    return jax.shard_map(f, mesh=mesh, in_specs=in_specs, out_specs=out_specs, check_vma=False)
```

```python
import functools

import jax
import jax.numpy as jnp
from jax import lax
from jax.experimental import pallas as pl
from jax.experimental.pallas import tpu as pltpu
from jax.sharding import PartitionSpec as P

F32, BF16 = jnp.float32, jnp.bfloat16
LANES = 128
VLIM = 60 * 1024 * 1024


def tile_of(n):
    for t in (512, 384, 256, 128):
        if n % t == 0:
            return t
    return n


def flip(i, d):
    out, b = i, 1
    while b <= d:
        if d & b:
            out = out + b * (1 - 2 * ((i // b) % 2))
        b *= 2
    return out


def remote(src, dst, send, recv, g, e):
    return pltpu.make_async_remote_copy(
        src_ref=src, dst_ref=dst, send_sem=send, recv_sem=recv,
        device_id={"grp": g, "seq": e}, device_id_type=pl.DeviceIdType.MESH,
    )


def kernel(G, S, tok_h, rt_h, gain_h, wi_h, wo_h, eo, wts,
           tok, rt, gain, wi, wo, logits, dT, pf, pb, xb, hp, hpc, hz, hzc, cown, sb, zb,
           ninv, acc, gath, hid, part, rs, eown,
           loc, a_s, a_r, f_s, f_r, p_s, p_r, h_s, h_r, z_s, z_r, zh_s, zh_r,
           n_s, n_r, i_s, i_r, r_s, r_r, e_s, e_r, ef_s, ef_r):
    g, e = lax.axis_index("grp"), lax.axis_index("seq")
    Z = S // 2
    z, k = e // 2, e % 2
    partner = e + 1 - 2 * k
    rows = rt_h.shape[0]
    half = rows // 2
    T, D = tok.shape
    SL = rt.shape[1]
    E = SL // S
    FF = wi.shape[1]
    tn = tile_of(D)
    NT = D // tn
    tf = tile_of(FF)
    cols = [pl.ds(t * tn, tn) for t in range(NT)]

    def rsl(gg, kk):
        return pl.ds(pl.multiple_of(gg * rows + kk * half, 16), half)

    c_rt = pltpu.make_async_copy(rt_h, rt.at[pl.ds(pl.multiple_of(g * rows, 16), rows)], loc.at[0])
    c_tok = pltpu.make_async_copy(tok_h.at[0], tok, loc.at[1])
    c_wi = pltpu.make_async_copy(wi_h.at[0], wi, loc.at[2])
    c_wo = pltpu.make_async_copy(wo_h.at[0], wo, loc.at[3])
    c_rt.start()
    c_tok.start()
    c_gain = pltpu.make_async_copy(gain_h, gain, loc.at[4])
    c_gain.start()
    hp[...] = jnp.zeros_like(hp)
    hz[...] = jnp.zeros_like(hz)

    bar = pltpu.get_barrier_semaphore()

    def greet(gg, ee):
        pl.semaphore_signal(bar, inc=1, device_id={"grp": gg, "seq": ee},
                            device_id_type=pl.DeviceIdType.MESH)

    def gpeer(d):
        return flip(g, d)

    def gfrom(d):
        return flip(g, d)

    def chunk(gg):
        at = pl.ds(pl.multiple_of(gg * rows, LANES), rows)
        return jnp.dot(tok[:, at], rt[at, :], preferred_element_type=F32)

    def zpeer(d):
        return flip(z, d)

    def zfrom(d):
        return flip(z, d)

    greet(g, partner)
    for d in range(1, G):
        greet(gpeer(d), e)
    for d in range(1, Z):
        greet(g, zpeer(d) * 2 + k)
    pl.semaphore_wait(bar, G + Z - 1)

    pend = []

    ksl = pl.ds(pl.multiple_of(k * half, 16), half)
    for d in range(G - 1, 0, -1):
        c = remote(rt_h.at[ksl], rt.at[rsl(g, k)], a_s.at[d], a_r.at[d], gpeer(d), e)
        c.start()
        pend.append(c)
    c_wi.start()
    c_wo.start()
    for d in range(1, G):
        sl = rt.at[rsl(gfrom(d), k)]
        remote(sl, sl, a_s.at[d], a_r.at[d], g, partner).wait_recv()
        c = remote(sl, sl, f_s.at[d], f_r.at[d], g, partner)
        c.start()
        pend.append(c)
    if not rows % LANES:
        c_rt.wait()
        c_tok.wait()
        lg = chunk(g)
    for d in range(1, G):
        sl = rt.at[rsl(gfrom(d), 1 - k)]
        remote(sl, sl, f_s.at[d], f_r.at[d], g, partner).wait_recv()
        if not rows % LANES:
            lg = lg + chunk(gfrom(d))
    if rows % LANES:
        c_rt.wait()
        c_tok.wait()
        lg = jnp.dot(tok[...], rt[...], preferred_element_type=F32)
    high = jnp.max(lg, axis=0, keepdims=True)
    hp[0:1] = high
    c_h = remote(hp.at[pl.ds(0, 1)], hp.at[pl.ds(1, 1)], h_s, h_r, g, partner)
    c_h.start()
    pend.append(c_h)
    logits[...] = lg
    dT[...] = jnp.transpose(jnp.exp(lg - high)).astype(BF16)

    pair = []
    for t in range(NT):
        ps = jnp.dot(dT[...], tok[:, cols[t]], preferred_element_type=F32).reshape(Z, 2, E, tn)
        pf[:, :, :, cols[t]] = ps
        pb[:, :, :, cols[t]] = ps.astype(BF16)
        c = remote(pb.at[:, 1 - k, :, cols[t]], xb.at[:, :, cols[t]], p_s.at[t], p_r.at[t], g, partner)
        c.start()
        pair.append(c)

    c_h.wait_recv()
    hh = hp[...]
    hm = jnp.maximum(hh[0:1], hh[1:2])
    hpc[...] = jnp.transpose(jnp.exp(jnp.minimum(hh - hm, 0.0))).reshape(Z, 2, E, LANES)
    hz[0:1] = hm
    for d in range(1, Z):
        c = remote(hz.at[pl.ds(0, 1)], hz.at[pl.ds(d, 1)], zh_s.at[d], zh_r.at[d], g, zpeer(d) * 2 + k)
        c.start()
        pend.append(c)
    for t in range(NT):
        pair[t].wait_recv()
        for d in range(Z - 1, -1, -1):
            zz = zpeer(d)
            fac = hpc[zz, k]
            v = pf[zz, k, :, cols[t]] * fac[:, 0:1] + xb[zz, :, cols[t]].astype(F32) * fac[:, 1:2]
            if d == 0:
                cown[:, cols[t]] = v
            else:
                sb[d, :, cols[t]] = v.astype(BF16)
                c = remote(sb.at[d, :, cols[t]], zb.at[d, :, cols[t]], z_s.at[d, t], z_r.at[d, t],
                           g, zz * 2 + k)
                c.start()
                pend.append(c)
    for c in pair:
        c.wait_send()

    lg = logits[...]
    ex = jnp.exp(lg - jnp.max(lg, axis=1, keepdims=True))
    wts[...] = (ex / jnp.sum(ex, axis=1, keepdims=True)).astype(BF16)

    for d in range(1, Z):
        sl = hz.at[pl.ds(d, 1)]
        remote(sl, sl, zh_s.at[d], zh_r.at[d], g, e).wait_recv()
    hh = hz[...]
    top = jnp.max(hh[0:Z], axis=0, keepdims=True)
    hzc[...] = jnp.transpose(jnp.exp(jnp.minimum(hh - top, 0.0))).reshape(S, E, LANES)
    fac = hzc[e]
    sq = jnp.zeros((E, 1), F32)
    c_gain.wait()
    for t in range(NT):
        v = cown[:, cols[t]] * fac[:, 0:1]
        for d in range(1, Z):
            sl = zb.at[d, :, cols[t]]
            remote(sl, sl, z_s.at[d, t], z_r.at[d, t], g, e).wait_recv()
            v = v + zb[d, :, cols[t]].astype(F32) * fac[:, d:d + 1]
        gath[g, :, cols[t]] = (v * gain[:, cols[t]]).astype(BF16)
        sl = gath.at[g, :, cols[t]]
        for d in range(G - 1, 0, -1):
            c = remote(sl, sl, n_s.at[d, t], n_r.at[d, t], gpeer(d), e)
            c.start()
            pend.append(c)
        sq = sq + jnp.sum(v * v, axis=1, keepdims=True)
    ninv[g] = jnp.broadcast_to(lax.rsqrt(sq / D + 1e-06), (E, LANES))
    for d in range(1, G):
        c = remote(ninv.at[g], ninv.at[g], i_s.at[d], i_r.at[d], gpeer(d), e)
        c.start()
        pend.append(c)
    c_wi.wait()
    c_wo.wait()
    for t in range(NT):
        for d in range(1, G):
            sl = gath.at[gfrom(d), :, cols[t]]
            remote(sl, sl, n_s.at[d, t], n_r.at[d, t], g, e).wait_recv()
        x = gath[:, :, cols[t]].reshape(G * E, tn)
        if t == NT - 1:
            for d in range(1, G):
                sl = ninv.at[gfrom(d)]
                remote(sl, sl, i_s.at[d], i_r.at[d], g, e).wait_recv()
            inv = ninv[...].reshape(G * E, LANES)[:, 0:1]
        for f in range(FF // tf):
            fs = pl.ds(f * tf, tf)
            y = jnp.dot(x, wi[cols[t], fs], preferred_element_type=F32)
            if t:
                y = y + acc[:, fs]
            if t == NT - 1:
                hid[:, fs] = jax.nn.gelu(y * inv).astype(BF16)
            else:
                acc[:, fs] = y
    hd = hid[...]
    for t in range(NT):
        part[:, :, cols[t]] = jnp.dot(hd, wo[:, cols[t]], preferred_element_type=F32).astype(BF16).reshape(G, E, tn)
        for d in range(G - 1, 0, -1):
            c = remote(part.at[gpeer(d), :, cols[t]], rs.at[d, :, cols[t]], r_s.at[d, t], r_r.at[d, t],
                       gpeer(d), e)
            c.start()
            pend.append(c)

    own = []
    for t in range(NT):
        v = part[g, :, cols[t]].astype(F32)
        for d in range(1, G):
            sl = rs.at[d, :, cols[t]]
            remote(sl, sl, r_s.at[d, t], r_r.at[d, t], g, e).wait_recv()
            v = v + rs[d, :, cols[t]].astype(F32)
        eown[:, cols[t]] = v.astype(BF16)
        src, dst = eown.at[:, cols[t]], eo.at[e, :, cols[t]]
        for d in range(Z - 1, 0, -1):
            c = remote(src, dst, e_s.at[d, t], e_r.at[d, t], g, zpeer(d) * 2 + k)
            c.start()
            pend.append(c)
        c = remote(src, dst, ef_s.at[0, t], ef_r.at[0, t], g, partner)
        c.start()
        pend.append(c)
        c = pltpu.make_async_copy(src, dst, e_s.at[0, t])
        c.start()
        own.append(c)
    for t in range(NT):
        for d in range(1, Z):
            sl = eo.at[zfrom(d) * 2 + k, :, cols[t]]
            remote(sl, sl, e_s.at[d, t], e_r.at[d, t], g, e).wait_recv()
            c = remote(sl, sl, ef_s.at[d, t], ef_r.at[d, t], g, partner)
            c.start()
            pend.append(c)
    for t in range(NT):
        own[t].wait()
        for d in range(Z):
            sl = eo.at[zfrom(d) * 2 + 1 - k, :, cols[t]]
            remote(sl, sl, ef_s.at[d, t], ef_r.at[d, t], g, e).wait_recv()
    for c in pend:
        c.wait_send()


def local(G, S, tokens, router, norm_gain, w_in, w_out):
    _, T, D = tokens.shape
    rows, SL = router.shape
    E, Z = SL // S, S // 2
    FF = w_in.shape[2]
    NT = D // tile_of(D)
    anyspace = pl.BlockSpec(memory_space=pl.ANY)
    hbm = pl.BlockSpec(memory_space=pltpu.HBM)
    vmem = pl.BlockSpec(memory_space=pltpu.VMEM)
    dma = lambda *s: pltpu.SemaphoreType.DMA(s)
    eo, wts = pl.pallas_call(
        functools.partial(kernel, G, S),
        out_shape=(jax.ShapeDtypeStruct((S, E, D), BF16), jax.ShapeDtypeStruct((T, SL), BF16)),
        in_specs=[hbm] * 5,
        out_specs=(anyspace, vmem),
        scratch_shapes=[
            pltpu.VMEM((T, D), BF16),
            pltpu.VMEM((rows * G, SL), BF16),
            pltpu.VMEM((1, D), F32),
            pltpu.VMEM((D, FF), BF16),
            pltpu.VMEM((FF, D), BF16),
            pltpu.VMEM((T, SL), F32),
            pltpu.VMEM((SL, T), BF16),
            pltpu.VMEM((Z, 2, E, D), F32),
            pltpu.VMEM((Z, 2, E, D), BF16),
            pltpu.VMEM((Z, E, D), BF16),
            pltpu.VMEM((LANES, SL), F32),
            pltpu.VMEM((Z, 2, E, LANES), F32),
            pltpu.VMEM((LANES, SL), F32),
            pltpu.VMEM((S, E, LANES), F32),
            pltpu.VMEM((E, D), F32),
            pltpu.VMEM((Z, E, D), BF16),
            pltpu.VMEM((Z, E, D), BF16),
            pltpu.VMEM((G, E, LANES), F32),
            pltpu.VMEM((G * E, FF), F32),
            pltpu.VMEM((G, E, D), BF16),
            pltpu.VMEM((G * E, FF), BF16),
            pltpu.VMEM((G, E, D), BF16),
            pltpu.VMEM((G, E, D), BF16),
            pltpu.VMEM((E, D), BF16),
            dma(5), dma(G), dma(G), dma(G), dma(G), dma(NT), dma(NT),
            pltpu.SemaphoreType.DMA, pltpu.SemaphoreType.DMA,
            dma(Z, NT), dma(Z, NT), dma(Z), dma(Z),
            dma(G, NT), dma(G, NT), dma(G), dma(G), dma(G, NT), dma(G, NT),
            dma(Z, NT), dma(Z, NT), dma(Z, NT), dma(Z, NT),
        ],
        compiler_params=pltpu.CompilerParams(
            collective_id=0, has_side_effects=True, vmem_limit_bytes=VLIM
        ),
    )(tokens, router, norm_gain, w_in, w_out)
    mixed = jnp.dot(wts, eo.reshape(SL, D), preferred_element_type=F32)
    return (tokens[0].astype(F32) + mixed).astype(BF16)[None]


def solution(mesh):
    in_specs = (
        P("grp", "seq", None),
        P("grp", None),
        P("seq", None),
        P("seq", None, "grp"),
        P("seq", "grp", None),
    )
    out_specs = P("grp", "seq", None)
    f = functools.partial(local, mesh.shape["grp"], mesh.shape["seq"])
    return jax.shard_map(f, mesh=mesh, in_specs=in_specs, out_specs=out_specs, check_vma=False)
```
